32 devices in a mesh: seq: 8 (over z, x), vocab: 4 (over y, core).
Axes of the slice: x: 2, y: 2, z: 4, core: 2. Of those that a mesh axis runs over, the one named last changes fastest.
Arguments:
- hidden: bfloat16 [2, 1024, 2048], P(None, 'seq'), may hold values from -6 to 6
- embedded: bfloat16 [2, 1024, 2048], P(None, 'seq'), may hold values from -6 to 6
- targets: int32 [2, 1024], P(None, 'seq'), may hold values from 0 to 51199
- main_mask: int32 [2, 1024], P(None, 'seq'), may hold values 0 or 1
- mtp_mask: int32 [2, 1024], P(None, 'seq'), may hold values from 0 to 1, as said below
- lengths: int32 [2], replicated, may hold values from 256 to 1024, as said below
- head_weight: bfloat16 [2048, 51200], P(None, ('seq', 'vocab')), may hold values from -7.6733202 to 7.6733202
- projection: bfloat16 [4096, 2048], P(None, 'vocab'), may hold values from -0.09375 to 0.09375
- main_gain: float32 [2048], replicated, may hold values from 0.5 to 1.5
- hidden_gain: float32 [2048], replicated, may hold values from 0.5 to 1.5
- embed_gain: float32 [2048], replicated, may hold values from 0.5 to 1.5
- mtp_gain: float32 [2048], replicated, may hold values from 0.5 to 1.5
Outputs:
- main_tokens: float32 [2, 1024], P(None, 'seq')
- mtp_tokens: float32 [2, 1024], P(None, 'seq')
- total_loss: float32 [], replicated
The draws below stay inside these ranges and needn't reach their ends.
Inputs may be any that keep to these rules, and one draw needn't show every extreme that they name: `mtp_mask`: 1 at every position that is a multiple of 128. `lengths`: the first sequence has length 1024.
All inputs are finite; a program needn't handle non-finite values. No bound on the sum of `main_mask` on one device may be relied on, other than what follows from the above.
Results may differ from the reference program's by a relative error of at most 0.0004.
The reference program's roundings to bfloat16 on the way (of `main_rows`, `previous`, `joined`, `mixed` and `mtp_rows`) count: a program that leaves them out, or rounds other values in their place, can miss the bound.
Values may be sent and summed in bfloat16 or wider, within the bound.
A program may use at most 128 MiB of HBM per device.

```python
import math
import jax
import jax.numpy as jnp
import numpy as np
from jax import lax

D = 2048
VOCAB = 51200
TOK_DEV = 128
MICRO = 2
SEQ = 1024


def draw_head_weight(key, part):
    key_base = jax.random.fold_in(key, 1)
    result_draw = jnp.clip(jax.random.normal(key_base, (D, VOCAB), jnp.float32), -6.0, 6.0) * (3.0 / math.sqrt(D))
    return result_draw.astype(jnp.bfloat16)


def draw_lengths(key, part):
    drawn = jax.random.randint(jax.random.fold_in(key, 11), (MICRO,), SEQ // 4, SEQ + 1).astype(jnp.int32)
    return drawn.at[0].set(SEQ)


def draw_mtp_mask(key, part):
    levels = jax.random.randint(jax.random.fold_in(key, 23), (MICRO, SEQ), 0, 4)
    position = jnp.arange(SEQ, dtype=jnp.int32)[None, :]
    return jnp.where((position % TOK_DEV == 0) | (levels < 3), 1, 0).astype(jnp.int32)


def touch_ends(values, stream_key, smallest, high):
    extent = values.shape
    place = [jax.random.randint(jax.random.fold_in(stream_key, axis), (), 0, extent[axis]) for axis in range(len(extent))]
    values = values.at[tuple(place)].set(smallest)
    longest = extent.index(max(extent))
    place[longest] = (place[longest] + 1) % extent[longest]
    return values.at[tuple(place)].set(high)


def block_levels(key, shape, shards, least, high):
    gain, own = 1.0, jax.random.fold_in(key, 6)
    for axis_at, blocks in shards:
        draws = jnp.exp(jax.random.uniform(jax.random.fold_in(own, axis_at), (blocks,), jnp.float32, least / len(shards), high / len(shards)))
        gain = gain * jnp.repeat(draws, shape[axis_at] // blocks).reshape([-1 if axis == axis_at else 1 for axis in range(len(shape))])
    return gain


def rank_bounds(count, slope):
    weights = [(1 << 20) // math.isqrt(standing ** slope) + 1 for standing in range(1, count + 1)]
    scale = 1 + sum(weights) // (1 << 30)
    return np.cumsum(np.array([max(1, weight // scale) for weight in weights]))


def ranked(key, dims, number_of, lean):
    table = rank_bounds(number_of, lean)
    ticket = jax.random.randint(jax.random.fold_in(key, 1), dims, 0, int(table[number_of - 1]))
    rank = jnp.searchsorted(jnp.asarray(table, jnp.int32), ticket, side="right")
    return jax.random.permutation(jax.random.fold_in(key, 2), number_of)[rank].astype(jnp.int32)


def scatter_about(key, shape, deviation, limit, cuts=(), kind=jnp.bfloat16):
    loudness = block_levels(key, shape, cuts, -0.22, 0.18) if cuts else 1.0
    result = jax.random.normal(key, shape, jnp.float32) * deviation * loudness
    return jnp.minimum(jnp.maximum(result, -limit), limit).astype(kind)


def setup_inputs(seed: int = 0) -> dict:
    streams_of = jax.random.split(jax.random.key(seed), 13)
    hidden = scatter_about(streams_of[0], (MICRO, SEQ, D), 1.0, 6.0, ((1, 8),))
    embedded = scatter_about(streams_of[1], (MICRO, SEQ, D), 1.0, 6.0, ((1, 8),))
    targets = touch_ends(ranked(streams_of[2], (MICRO, SEQ), VOCAB, 2), jax.random.fold_in(streams_of[2], 3), 0, VOCAB - 1).astype(jnp.int32)
    main_mask = touch_ends((jax.random.randint(streams_of[3], (MICRO, SEQ), 0, 4) < 3).astype(jnp.int32), jax.random.fold_in(streams_of[3], 1), 0, 1)
    mtp_mask = draw_mtp_mask(jax.random.fold_in(streams_of[12], 71), 0)
    lengths = draw_lengths(jax.random.fold_in(streams_of[12], 71), 0)
    head_weight = draw_head_weight(jax.random.fold_in(streams_of[12], 71), 0)
    projection = scatter_about(streams_of[7], (2 * D, D), (2 * D) ** -0.5, 0.09375, ((1, 4),))
    main_gain = jnp.clip(1.0 + 0.1 * jax.random.normal(streams_of[8], (D,), jnp.float32), 0.5, 1.5)
    hidden_gain = jnp.clip(1.0 + 0.1 * jax.random.normal(streams_of[9], (D,), jnp.float32), 0.5, 1.5)
    embed_gain = jnp.clip(1.0 + 0.1 * jax.random.normal(streams_of[10], (D,), jnp.float32), 0.5, 1.5)
    mtp_gain = jnp.clip(1.0 + 0.1 * jax.random.normal(streams_of[11], (D,), jnp.float32), 0.5, 1.5)
    return {"hidden": hidden, "embedded": embedded, "targets": targets, "main_mask": main_mask, "mtp_mask": mtp_mask, "lengths": lengths, "head_weight": head_weight, "projection": projection, "main_gain": main_gain, "hidden_gain": hidden_gain, "embed_gain": embed_gain, "mtp_gain": mtp_gain}


EPSILON = 1e-06
MTP_WEIGHT = 0.3

def normalize(values, gain_vec):
    values = values.astype(jnp.float32)
    mean_square = lax.optimization_barrier(jnp.mean(values * values, axis=-1, keepdims=True))
    return values * lax.rsqrt(mean_square + EPSILON) * gain_vec.astype(jnp.float32)

def cross_entropy(all_rows, wanted, head_weight):
    block_size = math.gcd(512, all_rows.shape[0])
    grouped = all_rows.reshape(-1, block_size, all_rows.shape[1])
    grouped_ids = wanted.reshape(-1, block_size)

    def one_block(block_pair):
        block_rows, block_ids = block_pair
        logits = jnp.dot(block_rows, head_weight, preferred_element_type=jnp.float32)
        highest = lax.optimization_barrier(jnp.max(logits, axis=1))
        exp_total = lax.optimization_barrier(jnp.sum(jnp.exp(logits - highest[:, None]), axis=1))
        target_logit = jnp.take_along_axis(logits, block_ids[:, None].astype(jnp.int32), axis=1)[:, 0]
        return highest + jnp.log(exp_total) - target_logit
    return lax.map(one_block, (grouped, grouped_ids)).reshape(-1)

def reference(hidden, embedded, targets, main_mask, mtp_mask, lengths, head_weight, projection, main_gain, hidden_gain, embed_gain, mtp_gain):
    batches, seq_len, model_width = hidden.shape
    positions = jnp.arange(seq_len, dtype=jnp.int32)[None, :]
    length_col = lengths[:, None]
    keep_main = ((main_mask == 1) & (positions + 1 < length_col)).astype(jnp.float32)
    keep_mtp = ((mtp_mask == 1) & (positions >= 1) & (positions + 1 < length_col)).astype(jnp.float32)
    main_rows = normalize(hidden, main_gain).astype(jnp.bfloat16).reshape(-1, model_width)
    previous = jnp.concatenate([jnp.zeros((batches, 1, model_width), hidden.dtype), hidden[:, :-1, :]], axis=1)
    joined = jnp.concatenate([normalize(previous, hidden_gain), normalize(embedded, embed_gain)], axis=2)
    joined = joined.astype(jnp.bfloat16).reshape(-1, 2 * model_width)
    mixed = jnp.dot(joined, projection, preferred_element_type=jnp.float32).astype(jnp.bfloat16)
    mtp_rows = normalize(mixed, mtp_gain).astype(jnp.bfloat16)
    flat_targets = targets.reshape(-1)
    main_losses = cross_entropy(main_rows, flat_targets, head_weight).reshape(batches, seq_len)
    mtp_losses = cross_entropy(mtp_rows, flat_targets, head_weight).reshape(batches, seq_len)
    main_tokens = keep_main * main_losses
    mtp_tokens = keep_mtp * mtp_losses
    total_loss = jnp.sum(main_tokens) / jnp.maximum(jnp.sum(keep_main), 1.0) + MTP_WEIGHT * jnp.sum(mtp_tokens) / jnp.maximum(jnp.sum(keep_mtp), 1.0)
    return (main_tokens, mtp_tokens, total_loss)
```

```python
import functools

import jax
import jax.numpy as jnp
from jax import lax
from jax.experimental import pallas as pl
from jax.experimental.pallas import tpu as pltpu
from jax.sharding import PartitionSpec as P

EPSILON = 1e-06
MTP_WEIGHT = 0.3
CHUNK = 640


def from_behind(block, axis, distance):
    devices = range(lax.axis_size(axis))
    route = [(i - distance, i) for i in devices if i - distance in devices]
    return lax.ppermute(block, axis, route)


def normalize(values, gain_vec):
    values = values.astype(jnp.float32)
    mean_square = jnp.mean(values * values, axis=-1, keepdims=True)
    return values * lax.rsqrt(mean_square + EPSILON) * gain_vec


def join_stats(earlier, latter):
    highest = jnp.maximum(earlier[0], latter[0])
    exp_total = earlier[1] * jnp.exp(earlier[0] - highest) + latter[1] * jnp.exp(
        latter[0] - highest
    )
    return (highest, exp_total, earlier[2] + latter[2])


def seq_perm(value, bit):
    pairs = [(i, i ^ (1 << bit)) for i in range(lax.axis_size("seq"))]
    return lax.ppermute(value, "seq", pairs)


def vocab_perm(value, bit):
    pairs = [(i, i ^ (1 << bit)) for i in range(lax.axis_size("vocab"))]
    return lax.ppermute(value, "vocab", pairs)


def bits_of(axis):
    return list(reversed(range(lax.axis_size(axis).bit_length() - 1)))


def gather_pieces(own):
    pieces = [own]
    for bit in bits_of("seq"):
        held = pieces[0] if len(pieces) == 1 else jnp.concatenate(pieces, axis=0)
        pieces.append(seq_perm(held, bit))
    return pieces


def head_kernel(masks, at_ref, *refs):
    blocks = refs[: len(masks)]
    gain_ref, local_ref, w_ref, out_ref, rows_ref = refs[len(masks) :]
    rows, width = rows_ref.shape
    part = blocks[0].shape[2]
    values = [block[0].astype(jnp.float32) for block in blocks]
    square = sum(jnp.sum(v * v, axis=1, keepdims=True) for v in values)
    scale = lax.rsqrt(square / width + EPSILON)
    for mask, value in zip(masks, values):
        place = pl.ds(pl.multiple_of((at_ref[0] ^ mask) * part, part), part)
        rows_ref[:, place] = (value * scale * gain_ref[:, place]).astype(jnp.bfloat16)
    wanted = local_ref[0]
    cols = w_ref.shape[1]
    stats = None
    for start in range(0, cols, CHUNK):
        stop = min(start + CHUNK, cols)
        logits = jnp.dot(
            rows_ref[...], w_ref[:, start:stop], preferred_element_type=jnp.float32
        )
        ids = lax.broadcasted_iota(jnp.int32, logits.shape, 1) + start
        highest = jnp.max(logits, axis=1, keepdims=True)
        total = jnp.sum(jnp.exp(logits - highest), axis=1, keepdims=True)
        picked = jnp.sum(jnp.where(ids == wanted, logits, 0.0), axis=1, keepdims=True)
        fresh = (highest, total, picked)
        stats = fresh if stats is None else join_stats(stats, fresh)
    lane = lax.broadcasted_iota(jnp.int32, (rows, 128), 1)
    packed = jnp.where(lane == 0, stats[0], jnp.where(lane == 1, stats[1], stats[2]))
    out_ref[0] = packed.T[:8]


def head_stats(masks, at, blocks, gain, local, head_weight):
    count, rows, part = blocks[0].shape
    width, cols = head_weight.shape
    flops = 2 * count * rows * width * cols
    return pl.pallas_call(
        functools.partial(head_kernel, masks),
        out_shape=jax.ShapeDtypeStruct((count, 8, rows), jnp.float32),
        grid_spec=pltpu.PrefetchScalarGridSpec(
            num_scalar_prefetch=1,
            grid=(count,),
            in_specs=[pl.BlockSpec((1, rows, part), lambda i, at: (i, 0, 0)) for _ in blocks]
            + [
                pl.BlockSpec((1, width), lambda i, at: (0, 0)),
                pl.BlockSpec((1, rows, 1), lambda i, at: (i, 0, 0)),
                pl.BlockSpec((width, cols), lambda i, at: (0, 0)),
            ],
            out_specs=pl.BlockSpec((1, 8, rows), lambda i, at: (i, 0, 0)),
            scratch_shapes=[pltpu.VMEM((rows, width), jnp.bfloat16)],
        ),
        compiler_params=pltpu.CompilerParams(vmem_limit_bytes=48 * 2**20),
        cost_estimate=pl.CostEstimate(
            flops=flops, bytes_accessed=2 * (width * cols + count * rows * width), transcendentals=count * rows * cols
        ),
    )(at, *blocks, gain.reshape(1, -1), local, head_weight)


def join_packed(a, b):
    joined = join_stats((a[:, 0], a[:, 1], a[:, 2]), (b[:, 0], b[:, 1], b[:, 2]))
    return jnp.stack(joined, axis=1)


def finish(packed):
    held = packed[:, :3]
    for bit in reversed(bits_of("seq")):
        half = held.shape[0] // 2
        held = join_packed(held[:half], seq_perm(held[half:], bit))
    for bit in bits_of("vocab"):
        held = join_packed(held, vocab_perm(held, bit))
    return held[0, 0] + jnp.log(held[0, 1]) - held[0, 2]


def shards(
    hidden,
    embedded,
    targets,
    main_mask,
    mtp_mask,
    lengths,
    head_weight,
    projection,
    main_gain,
    hidden_gain,
    embed_gain,
    mtp_gain,
):
    batches, seq_len, model_width = hidden.shape
    rows = batches * seq_len
    seq_index = lax.axis_index("seq")
    vocab_index = lax.axis_index("vocab")
    vocab_count = lax.axis_size("vocab")
    cols = head_weight.shape[1]

    incoming = from_behind(hidden[:, seq_len - 1 :, :], "seq", 1)

    core = vocab_index & 1
    half = model_width // 2
    flat = hidden.reshape(1, rows, model_width)
    mine = lax.dynamic_slice_in_dim(flat, core * half, half, axis=2)
    other = lax.dynamic_slice_in_dim(flat, (1 - core) * half, half, axis=2)
    main_pieces = gather_pieces(mine)
    main_other = [other] + [vocab_perm(piece, 0) for piece in main_pieces[1:]]
    main_blocks = [jnp.concatenate(p, axis=0) for p in (main_pieces, main_other)]

    wanted = jnp.concatenate(gather_pieces(targets.reshape(1, rows)), axis=0)
    local = (wanted - (seq_index * vocab_count + vocab_index) * cols)[:, :, None]

    previous = jnp.concatenate([incoming, hidden[:, : seq_len - 1, :]], axis=1)
    joined = jnp.concatenate(
        [normalize(previous, hidden_gain), normalize(embedded, embed_gain)], axis=2
    )
    joined = joined.astype(jnp.bfloat16).reshape(rows, 2 * model_width)
    mixed = jnp.dot(joined, projection, preferred_element_type=jnp.float32).astype(jnp.bfloat16)
    masks = [0]
    held = [gather_pieces(mixed[None])]
    for bit in bits_of("vocab"):
        masks = masks + [mask | (1 << bit) for mask in masks]
        held = held + [[vocab_perm(piece, bit) for piece in pieces] for pieces in held]
    mtp_blocks = [jnp.concatenate(pieces, axis=0) for pieces in held]

    main_stats = head_stats((0, 1), core[None], main_blocks, main_gain, local, head_weight)
    mtp_stats = head_stats(tuple(masks), vocab_index[None], mtp_blocks, mtp_gain, local, head_weight)

    positions = seq_index * seq_len + lax.broadcasted_iota(jnp.int32, (batches, seq_len), 1)
    inside = positions + 1 < lengths[:, None]
    keep_main = ((main_mask == 1) & inside).astype(jnp.float32)
    keep_mtp = ((mtp_mask == 1) & (positions >= 1) & inside).astype(jnp.float32)
    main_tokens = keep_main * finish(main_stats).reshape(batches, seq_len)
    mtp_tokens = keep_mtp * finish(mtp_stats).reshape(batches, seq_len)
    sums = jnp.stack(
        [jnp.sum(main_tokens), jnp.sum(mtp_tokens), jnp.sum(keep_main), jnp.sum(keep_mtp)]
    )
    for bit in bits_of("seq"):
        sums = sums + seq_perm(sums, bit)
    total_loss = sums[0] / jnp.maximum(sums[2], 1.0) + MTP_WEIGHT * sums[1] / jnp.maximum(
        sums[3], 1.0
    )
    return (main_tokens, mtp_tokens, total_loss)


def solution(mesh):
    return jax.shard_map(
        shards,
        mesh=mesh,
        in_specs=(
            P(None, "seq", None),
            P(None, "seq", None),
            P(None, "seq"),
            P(None, "seq"),
            P(None, "seq"),
            P(),
            P(None, ("seq", "vocab")),
            P(None, "vocab"),
            P(),
            P(),
            P(),
            P(),
        ),
        out_specs=(P(None, "seq"), P(None, "seq"), P()),
        check_vma=False,
    )
```
